32 devices in a mesh: groups: 2 (over y), tm: 4 (over z), chan: 2 (over x), night: 2 (over core).
Axes of the slice: x: 2, y: 2, z: 4, core: 2. Of those that a mesh axis runs over, the one named last changes fastest.
Arguments:
- signal: bfloat16 [4, 1024, 8192], P(('groups', 'night'), 'tm', 'chan'), parts along dimension 0, may hold values from -6 to 6
- lengths: int32 [4], P(('groups', 'night')), parts along dimension 0, may hold values from 256 to 1024, as said below
- patch_weight: bfloat16 [256, 1024], replicated
- chan_embed: float32 [32, 1024], P('chan'), may hold values from -5 to 5
- ln_gain: float32 [1024], replicated, may hold values from 0.1 to 1.9
- qkv_weight: bfloat16 [3, 1024, 1024], P(None, None, 'chan'), may hold values from -0.1875 to 0.1875
- head_temp: float32 [16], P('chan'), may hold values from 0.8 to 3
- out_weight: bfloat16 [1024, 1024], P('chan'), may hold values from -0.1875 to 0.1875
Outputs:
- encoded: bfloat16 [4, 1024, 1024], P(('groups', 'night'), 'tm', 'chan'), parts along dimension 0
The draws below stay inside these ranges and needn't reach their ends.
There are 2 independent parts, one for each index of `groups`. The reference program is written for one: setup_inputs(seed, part) draws one part's arguments, and reference() takes and returns one part's arrays. A program takes and returns all parts, laid end to end along the dimension named above; an argument that names none is the same for every part. Nothing has to cross between parts.
Inputs may be any that keep to these rules, and one draw needn't show every extreme that they name: `lengths`: each night's number of valid tokens; in every draw some night is complete (1024 tokens).
All inputs are finite; a program needn't handle non-finite values.
Results may differ from the reference program's by a relative error of at most 0.0037.
Values may be sent and summed in bfloat16 or wider, within the bound.
A program may use at most 64 MiB of HBM per device.

```python
import math
import jax
import jax.numpy as jnp
from jax import lax

CH = 32
PATCH = 256
D = 1024
H = 16
HD = 64
WINDOW = 1024
TOK_DEV = 256
SEQ = 1024
NIGHTS = 2


def draw_lengths(key, part):
    first_key, second_key = jax.random.split(key)
    drawn = jax.random.randint(first_key, (NIGHTS,), SEQ // 4, SEQ + 1)
    full_night = jax.random.randint(second_key, (), 0, NIGHTS)
    return jnp.where(jnp.arange(NIGHTS) == full_night, SEQ, drawn).astype(jnp.int32)


def draw_patch_weight(key, part):
    column = jnp.arange(D, dtype=jnp.float32) / (D - 1)
    ramp = jnp.exp(jnp.log(4.0) * column)
    base = jax.random.normal(key, (PATCH, D), jnp.float32)
    return (base * ramp * PATCH ** (-0.5)).astype(jnp.bfloat16)


def block_levels(rng, shape, cuts, low, high):
    def one(position, blocks):
        draws = jax.random.uniform(jax.random.fold_in(jax.random.fold_in(rng, 6), position), (blocks,), jnp.float32, low / len(cuts), high / len(cuts))
        return jnp.repeat(jnp.exp(draws), shape[position] // blocks).reshape((-1,) + (1,) * (len(shape) - position - 1))

    gain = one(*cuts[0])
    for cut in cuts[1:]:
        gain = gain * one(*cut)
    return gain


def scatter_about(rng, extent, scale, most, shards=(), held_as=jnp.bfloat16):
    values = jax.random.normal(rng, extent, jnp.float32) * scale
    if len(shards) > 0:
        values = block_levels(rng, extent, shards, -0.22, 0.18) * values
    return jnp.clip(values, min=-most, max=most).astype(held_as)


def setup_inputs(seed: int = 0, part: int = 0) -> dict:
    streams_of = jax.random.split(jax.random.key(seed), 9)
    part_splits = jax.random.split(jax.random.fold_in(streams_of[8], part), 9)
    signal = scatter_about(part_splits[0], (NIGHTS, SEQ, CH * PATCH), 1.0, 6.0, ((0, 2), (1, 4), (2, 2)))
    lengths = draw_lengths(jax.random.fold_in(jax.random.fold_in(streams_of[8], part), 71), part)
    patch_weight = draw_patch_weight(jax.random.fold_in(streams_of[8], 71), part)
    chan_embed = scatter_about(streams_of[3], (CH, D), 1.0, 5.0, ((0, 2),), jnp.float32)
    ln_gain = jnp.clip(1.0 + 0.18 * jax.random.normal(streams_of[4], (D,), jnp.float32), 0.1, 1.9)
    qkv_weight = scatter_about(streams_of[5], (3, D, H * HD), D ** -0.5, 0.1875, ((2, 2),))
    head_temp = jnp.clip(jnp.exp(math.log(3.0) - 1.3217558 * jax.random.uniform(streams_of[6], (H,), jnp.float32) ** block_levels(streams_of[6], (H,), ((0, 2),), -0.2, 0.2)), 0.8, 3.0)
    out_weight = scatter_about(streams_of[7], (H * HD, D), (H * HD) ** -0.5, 0.1875, ((0, 2),))
    return {"signal": signal, "lengths": lengths, "patch_weight": patch_weight, "chan_embed": chan_embed, "ln_gain": ln_gain, "qkv_weight": qkv_weight, "head_temp": head_temp, "out_weight": out_weight}


def unit_scale(values):
    return values * lax.rsqrt(lax.optimization_barrier(jnp.mean(values * values, axis=-1, keepdims=True)) + 1e-06)

def one_night(frames, night_len, patch_weight, chan_embed, ln_gain, qkv_weight, head_temp, out_weight):
    pooled = jnp.zeros((SEQ, D), jnp.float32)
    for channel in range(CH):
        inputs = frames[:, channel * PATCH:(channel + 1) * PATCH]
        pre_act = jnp.dot(inputs, patch_weight, preferred_element_type=jnp.float32) + chan_embed[channel]
        pooled = pooled + jax.nn.gelu(pre_act)
    pooled = pooled / CH
    center = pooled - lax.optimization_barrier(jnp.mean(pooled, axis=-1, keepdims=True))
    spread = lax.optimization_barrier(jnp.mean(center * center, axis=-1, keepdims=True))
    normed = (center * lax.rsqrt(spread + 1e-05) * ln_gain).astype(jnp.bfloat16)
    query_all = jnp.dot(normed, qkv_weight[0], preferred_element_type=jnp.float32)
    key_all = jnp.dot(normed, qkv_weight[1], preferred_element_type=jnp.float32)
    value_all = jnp.dot(normed, qkv_weight[2], preferred_element_type=jnp.float32)
    queries = unit_scale(query_all.reshape(SEQ, H, HD)).astype(jnp.bfloat16)
    keys = unit_scale(key_all.reshape(SEQ, H, HD)).astype(jnp.bfloat16)
    values = value_all.reshape(SEQ, H, HD).astype(jnp.bfloat16)
    padded_keys = jnp.pad(keys, ((WINDOW, WINDOW), (0, 0), (0, 0)))
    padded_values = jnp.pad(values, ((WINDOW, WINDOW), (0, 0), (0, 0)))
    temp_scaled = head_temp * HD ** (-0.5)

    def block_attend(index):
        first = index * TOK_DEV
        query_blk = lax.dynamic_slice_in_dim(queries, first, TOK_DEV, 0)
        key_blk = lax.dynamic_slice_in_dim(padded_keys, first, TOK_DEV + 2 * WINDOW, 0)
        value_blk = lax.dynamic_slice_in_dim(padded_values, first, TOK_DEV + 2 * WINDOW, 0)
        query_pos = first + jnp.arange(TOK_DEV, dtype=jnp.int32)
        key_pos = first - WINDOW + jnp.arange(TOK_DEV + 2 * WINDOW, dtype=jnp.int32)
        allowed = (key_pos[None, :] >= 0) & (key_pos[None, :] < night_len) & (jnp.abs(query_pos[:, None] - key_pos[None, :]) <= WINDOW)
        row_live = query_pos < night_len
        scores = jnp.einsum('qhd,khd->hqk', query_blk.astype(jnp.float32), key_blk.astype(jnp.float32)) * temp_scaled[:, None, None]
        raised = jnp.where(allowed[None], jnp.exp(scores), 0.0)
        totals = jnp.where(row_live[None], lax.optimization_barrier(jnp.sum(raised, axis=-1)), 1.0)
        attn_weights = (raised / totals[..., None]).astype(jnp.bfloat16)
        mixed = jnp.einsum('hqk,khd->qhd', attn_weights.astype(jnp.float32), value_blk.astype(jnp.float32))
        return mixed.reshape(TOK_DEV, H * HD).astype(jnp.bfloat16)
    attended = lax.map(block_attend, jnp.arange(SEQ // TOK_DEV, dtype=jnp.int32)).reshape(SEQ, H * HD)
    branch = jnp.dot(attended, out_weight, preferred_element_type=jnp.float32)
    live_rows = jnp.arange(SEQ, dtype=jnp.int32) < night_len
    return jnp.where(live_rows[:, None], pooled + branch, 0.0).astype(jnp.bfloat16)

def reference(signal, lengths, patch_weight, chan_embed, ln_gain, qkv_weight, head_temp, out_weight):
    results = []
    for night_idx in range(NIGHTS):
        results.append(one_night(signal[night_idx], lengths[night_idx], patch_weight, chan_embed, ln_gain, qkv_weight, head_temp, out_weight))
    return jnp.stack(results)
```

```python
import functools
import math

import jax
import jax.numpy as jnp
from jax import lax
from jax.experimental import pallas as pl
from jax.experimental.pallas import tpu as pltpu
from jax.sharding import PartitionSpec as P

CH = 32
HD = 64
WINDOW = 1024
LOADS = 4
CHUNKS = 8
SPLIT = 3
ITEMS = CHUNKS - SPLIT
LAG = 2
MESH = pl.DeviceIdType.MESH
GELU_A = math.sqrt(2.0 / math.pi)
GELU_B = GELU_A * 0.044715
LOG2E = math.log2(math.e)


def kernel(
    n, reach, far,
    lengths, temp, signal, patch_w, embed, gain, qkv_w, out_w,
    out,
    sig_v, pw_v, qkv_v, ow_v, part, send_p, recv_p, win, qz, acc, att, send_b, recv_b,
    load_sem, sig_sem, ps_sem, pr_sem, zs_sem, zr_sem, xs_sem, xr_sem, bs_sem, br_sem,
):
    me = lax.axis_index("tm")
    col = lax.axis_index("chan")
    other = 1 - col
    load_rows = sig_v.shape[1]
    tok = load_rows * LOADS
    rows = tok // CHUNKS
    per_load = CHUNKS // LOADS
    width = pw_v.shape[1]
    share = qkv_v.shape[2]
    heads = share // HD
    pairs = heads // 2
    patch = pw_v.shape[0]
    chans = embed.shape[0]
    f32, bf16 = jnp.float32, jnp.bfloat16

    def sig_copy(r):
        return pltpu.make_async_copy(
            signal.at[0, pl.ds(r * load_rows, load_rows), :], sig_v.at[r], sig_sem.at[r]
        )

    loads = [
        pltpu.make_async_copy(patch_w, pw_v, load_sem.at[0]),
        pltpu.make_async_copy(qkv_w, qkv_v, load_sem.at[1]),
        pltpu.make_async_copy(out_w, ow_v, load_sem.at[2]),
    ]
    barrier = pltpu.get_barrier_semaphore()
    pl.semaphore_signal(barrier, inc=1, device_id={"chan": other}, device_id_type=MESH)

    @pl.when(me > 0)
    def _():
        pl.semaphore_signal(barrier, inc=1, device_id={"tm": me - 1}, device_id_type=MESH)

    @pl.when(me < n - 1)
    def _():
        pl.semaphore_signal(barrier, inc=1, device_id={"tm": me + 1}, device_id_type=MESH)

    loads[0].start()
    for r in range(LOADS):
        sig_copy(r).start()
    loads[1].start()
    loads[2].start()

    def part_copy(r):
        return pltpu.make_async_remote_copy(
            src_ref=send_p.at[r], dst_ref=recv_p.at[r], send_sem=ps_sem.at[r],
            recv_sem=pr_sem.at[r], device_id={"chan": other}, device_id_type=MESH,
        )

    def slot_of(side, d):
        return 2 * (d - 1) + side + 1

    def source(side, d):
        return me - d if side == 0 else me + d

    def held(side, d):
        s = source(side, d)
        return (s >= 0) & (s < n)

    def sends(side, d):
        nxt = me + 1 if side == 0 else me - 1
        return held(side, d - 1) & (nxt >= 0) & (nxt < n)

    def row_of(j):
        return jnp.where(j < SPLIT, 2 * j + col, j + SPLIT)

    def z_copy(side, d, j):
        src = jnp.where(d == 1, 0, slot_of(side, d - 1))
        dst = slot_of(side, d)
        nxt = me + 1 if side == 0 else me - 1
        r = row_of(j)
        return pltpu.make_async_remote_copy(
            src_ref=win.at[src, r], dst_ref=win.at[dst, r], send_sem=zs_sem.at[dst, j],
            recv_sem=zr_sem.at[dst, j], device_id={"tm": nxt}, device_id_type=MESH,
        )

    def x_copy(slot, r, j):
        return pltpu.make_async_remote_copy(
            src_ref=win.at[slot, r], dst_ref=win.at[slot, r], send_sem=xs_sem.at[slot, j],
            recv_sem=xr_sem.at[slot, j], device_id={"chan": other}, device_id_type=MESH,
        )

    loads[0].wait()

    def patch_step(r):
        sig_copy(r).wait()
        half = width // 2

        def col_step(b, carry):
            cs = pl.ds(pl.multiple_of(b * half, half), half)
            w = pw_v[:, cs]
            total = jnp.zeros((load_rows, half), f32)
            for c0 in range(0, chans, 4):
                lhs = jnp.concatenate(
                    [sig_v[r, :, (c0 + c) * patch : (c0 + c + 1) * patch] for c in range(4)], axis=0
                )
                y4 = jnp.dot(lhs, w, preferred_element_type=f32)
                for c in range(4):
                    y = y4[c * load_rows : (c + 1) * load_rows] + embed[c0 + c : c0 + c + 1, cs]
                    t = jnp.tanh(y * (GELU_A + GELU_B * (y * y)))
                    total = total + (y + y * t)
            total = total * (0.5 / CH)
            for i in range(per_load):
                piece = total[i * rows : (i + 1) * rows]
                part[r * per_load + i, :, cs] = piece
                send_p[r * per_load + i, :, cs] = piece.astype(bf16)
            return carry

        lax.fori_loop(0, 2, col_step, 0)

        @pl.when(r == 0)
        def _():
            peers = 1 + jnp.where(me > 0, 1, 0) + jnp.where(me < n - 1, 1, 0)
            pl.semaphore_wait(barrier, peers)

        for i in range(per_load):
            part_copy(r * per_load + i).start()

    def norm_step(r):
        part_copy(r).wait_recv()
        pooled = part[r] + recv_p[r].astype(f32)
        part[r] = pooled
        center = pooled - jnp.mean(pooled, axis=-1, keepdims=True)
        spread = jnp.mean(center * center, axis=-1, keepdims=True)
        win[0, r] = (center * lax.rsqrt(spread + 1e-05) * gain[...]).astype(bf16)

        relay_out(r, 1)

    def handled(r):
        return (r >= 2 * SPLIT) | (lax.rem(r, 2) == col)

    def item_of(r):
        return jnp.where(r < 2 * SPLIT, r // 2, r - SPLIT)

    def relay_out(r, d):
        for side in range(2):
            @pl.when(handled(r) & sends(side, d))
            def _(side=side):
                z_copy(side, d, item_of(r)).start()

    def load_loop(r, carry):
        patch_step(r)
        return carry

    lax.fori_loop(0, LOADS, load_loop, 0)

    lane_block = lax.broadcasted_iota(jnp.int32, (256, 256), 0) // HD
    sub_block = lax.broadcasted_iota(jnp.int32, (256, 256), 1) // HD
    means = jnp.where(lane_block == sub_block, 1.0 / HD, 0.0).astype(bf16)
    low = lax.broadcasted_iota(jnp.int32, (tok, 2 * HD), 1) < HD

    def unit(x):
        outs = []
        for b in range(share // 256):
            y = x[:, b * 256 : (b + 1) * 256]
            ms = jnp.dot((y * y).astype(bf16), means, preferred_element_type=f32)
            outs.append((y * lax.rsqrt(ms + 1e-06)).astype(bf16))
        return jnp.concatenate(outs, axis=1)

    def project_queries():
        loads[1].wait()
        q = unit(jnp.dot(win[0].reshape(tok, width), qkv_v[0], preferred_element_type=f32))
        for p in range(pairs):
            qp = q[:, p * 2 * HD : (p + 1) * 2 * HD]
            zero = jnp.zeros_like(qp)
            qz[2 * p] = jnp.where(low, qp, zero)
            qz[2 * p + 1] = jnp.where(low, zero, qp)

    acc[...] = jnp.zeros_like(acc)
    valid_len = lengths[0]

    def attend(slot, src):
        x = win[slot].reshape(tok, width)
        k = unit(jnp.dot(x, qkv_v[1], preferred_element_type=f32))
        v = jnp.dot(x, qkv_v[2], preferred_element_type=f32)
        key_pos = src * tok + lax.broadcasted_iota(jnp.int32, (tok, 2 * HD), 0)
        ok = jnp.where(key_pos < valid_len, 1.0, 0.0)
        for p in range(pairs):
            kp = k[:, p * 2 * HD : (p + 1) * 2 * HD]
            vp = v[:, p * 2 * HD : (p + 1) * 2 * HD] * ok
            for h in range(2):
                rhs = jnp.where(low, vp, ok) if h == 0 else jnp.where(low, ok, vp)
                s = lax.dot_general(
                    qz[2 * p + h], kp, (((1,), (1,)), ((), ())), preferred_element_type=f32
                )
                e = jnp.exp2(s * (temp[2 * p + h] * (HD**-0.5 * LOG2E)))
                if far:
                    gap = (me - src) * tok + (
                        lax.broadcasted_iota(jnp.int32, (tok, tok), 0)
                        - lax.broadcasted_iota(jnp.int32, (tok, tok), 1)
                    )
                    e = jnp.where(jnp.abs(gap) <= WINDOW, e, 0.0)
                acc[2 * p + h] += jnp.dot(
                    e.astype(bf16), rhs.astype(bf16), preferred_element_type=f32
                )

    def relay(d, r):
        for side in range(2):
            @pl.when(handled(r) & held(side, d))
            def _(side=side):
                z_copy(side, d, item_of(r)).wait_recv()
                if d < reach:
                    @pl.when(sends(side, d + 1))
                    def _():
                        z_copy(side, d + 1, item_of(r)).start()

                @pl.when(r < 2 * SPLIT)
                def _():
                    x_copy(slot_of(side, d), r, item_of(r)).start()

    def attend_at(dist):
        def slot_step(i, c):
            src = jnp.where(i == 0, me - dist, me + dist)
            slot = jnp.where(dist == 0, 0, 2 * (dist - 1) + i + 1)

            @pl.when((src >= 0) & (src < n) & ((dist > 0) | (i == 0)))
            def _():
                @pl.when(dist > 0)
                def _():
                    for j in range(SPLIT):
                        x_copy(slot, 2 * j + other, j).wait_recv()

                attend(slot, src)

            return c

        lax.fori_loop(0, 2, slot_step, 0)

    def event(t, carry):
        @pl.when(t < CHUNKS)
        def _():
            norm_step(t)

        for d in range(1, reach + 1):
            r = t - LAG * d

            @pl.when((r >= 0) & (r < CHUNKS))
            def _(d=d, r=r):
                relay(d, r)

        late = t - CHUNKS + 1

        @pl.when((late >= 0) & (lax.rem(late, LAG) == 0))
        def _():
            @pl.when(late == 0)
            def _():
                project_queries()

            attend_at(late // LAG)

        return carry

    lax.fori_loop(0, CHUNKS + LAG * reach, event, 0)

    query_pos = me * tok + lax.broadcasted_iota(jnp.int32, (tok, 2 * HD), 0)
    live = query_pos < valid_len
    for p in range(pairs):
        a0, a1 = acc[2 * p], acc[2 * p + 1]
        num = jnp.where(low, a0, a1)
        den = pltpu.roll(jnp.where(low, a1, a0), HD, 1)
        den = jnp.where(live, den, 1.0)
        att[:, p * 2 * HD : (p + 1) * 2 * HD] = (num / den).astype(bf16)

    loads[2].wait()
    theirs = pl.ds(pl.multiple_of(other * share, share), share)
    mine = pl.ds(pl.multiple_of(col * share, share), share)

    def branch_copy(b):
        return pltpu.make_async_remote_copy(
            src_ref=send_b.at[b], dst_ref=recv_b.at[b], send_sem=bs_sem.at[b],
            recv_sem=br_sem.at[b], device_id={"chan": other}, device_id_type=MESH,
        )

    for b in range(2):
        a = att[b * (tok // 2) : (b + 1) * (tok // 2), :]
        send_b[b] = jnp.dot(a, ow_v[:, theirs], preferred_element_type=f32).astype(bf16)
        branch_copy(b).start()
    own = jnp.dot(att[...], ow_v[:, mine], preferred_element_type=f32)
    own = own + part[:, :, mine].reshape(tok, share)
    for b in range(2):
        rs = slice(b * (tok // 2), (b + 1) * (tok // 2))
        branch_copy(b).wait_recv()
        pos = me * tok + b * (tok // 2) + lax.broadcasted_iota(jnp.int32, (tok // 2, share), 0)
        total = own[rs] + recv_b[b].astype(f32)
        out[0, rs, :] = jnp.where(pos < valid_len, total, 0.0).astype(bf16)

    for r in range(CHUNKS):
        part_copy(r).wait_send()
    for b in range(2):
        branch_copy(b).wait_send()

    def drain(d, carry):
        for side in range(2):
            @pl.when(sends(side, d))
            def _(side=side):
                for j in range(ITEMS):
                    z_copy(side, d, j).wait_send()

            @pl.when(held(side, d))
            def _(side=side):
                for j in range(SPLIT):
                    x_copy(slot_of(side, d), 2 * j + col, j).wait_send()

        return carry

    lax.fori_loop(1, reach + 1, drain, 0)


GRAIN = 8
PIECES = ((0, 1), (1, 2), (2, 4), (4, 6), (6, 8))
DELAY = 3


def split_kernel(
    n,
    lengths, temp, signal, patch_w, embed, gain, qkv_w, out_w,
    out,
    sig_v, pw_v, qkv_v, ow_v, part, send_p, recv_p, normed, send_z, recv_z, qz, rhs, acc,
    send_a, recv_a, own_v, send_b, recv_b,
    load_sem, sig_sem, ps_sem, pr_sem, zs_sem, zr_sem, as_sem, ar_sem, bs_sem, br_sem,
):
    me = lax.axis_index("tm")
    col = lax.axis_index("chan")
    other = 1 - col
    rows = sig_v.shape[1]
    tok = rows * GRAIN
    width = pw_v.shape[1]
    share = qkv_v.shape[2]
    patch = pw_v.shape[0]
    chans = embed.shape[0]
    blocks = recv_z.shape[0]
    size = tok // blocks
    per_block = GRAIN // blocks
    pair = 2 * HD
    f32, bf16 = jnp.float32, jnp.bfloat16

    def sig_copy(r):
        return pltpu.make_async_copy(
            signal.at[0, pl.ds(r * rows, rows), :], sig_v.at[r], sig_sem.at[r]
        )

    loads = [
        pltpu.make_async_copy(patch_w, pw_v, load_sem.at[0]),
        pltpu.make_async_copy(qkv_w, qkv_v, load_sem.at[1]),
        pltpu.make_async_copy(out_w, ow_v, load_sem.at[2]),
    ]
    barrier = pltpu.get_barrier_semaphore()
    pl.semaphore_signal(barrier, inc=1, device_id={"chan": other}, device_id_type=MESH)
    for k in range(1, n):
        pl.semaphore_signal(
            barrier, inc=1, device_id={"tm": lax.rem(me + k, n)}, device_id_type=MESH
        )
    loads[0].start()
    for r in range(GRAIN):
        sig_copy(r).start()
    loads[1].start()
    loads[2].start()

    def part_copy(r):
        return pltpu.make_async_remote_copy(
            src_ref=send_p.at[r], dst_ref=recv_p.at[r], send_sem=ps_sem.at[r],
            recv_sem=pr_sem.at[r], device_id={"chan": other}, device_id_type=MESH,
        )

    def span(p):
        b, g = PIECES[p][0] // per_block, PIECES[p][0] % per_block
        return b, pl.ds(g * rows, (PIECES[p][1] - PIECES[p][0]) * rows)

    def z_send(p, dest):
        b, rs = span(p)
        return pltpu.make_async_remote_copy(
            src_ref=send_z.at[b, dest, :, rs], dst_ref=recv_z.at[b, :, me, rs],
            send_sem=zs_sem.at[p, dest], recv_sem=zr_sem.at[p, me],
            device_id={"tm": dest}, device_id_type=MESH,
        )

    def z_recv(p, src):
        b, rs = span(p)
        return pltpu.make_async_remote_copy(
            src_ref=send_z.at[b, src, :, rs], dst_ref=recv_z.at[b, :, src, rs],
            send_sem=zs_sem.at[p, src], recv_sem=zr_sem.at[p, src],
            device_id={"tm": src}, device_id_type=MESH,
        )

    def a_send(i, dest):
        return pltpu.make_async_remote_copy(
            src_ref=send_a.at[i, dest], dst_ref=recv_a.at[i, me], send_sem=as_sem.at[i, dest],
            recv_sem=ar_sem.at[i, me], device_id={"tm": dest}, device_id_type=MESH,
        )

    def a_recv(i, src):
        return pltpu.make_async_remote_copy(
            src_ref=send_a.at[i, src], dst_ref=recv_a.at[i, src], send_sem=as_sem.at[i, src],
            recv_sem=ar_sem.at[i, src], device_id={"tm": src}, device_id_type=MESH,
        )

    def b_copy(i):
        return pltpu.make_async_remote_copy(
            src_ref=send_b.at[i], dst_ref=recv_b.at[i], send_sem=bs_sem.at[i],
            recv_sem=br_sem.at[i], device_id={"chan": other}, device_id_type=MESH,
        )

    others = [lax.rem(me + k, n) for k in range(1, n)]
    loads[0].wait()
    group = 256 // rows

    def patch_step(r):
        sig_copy(r).wait()
        half = width // 2

        def col_step(b, carry):
            cs = pl.ds(pl.multiple_of(b * half, half), half)
            w = pw_v[:, cs]
            total = jnp.zeros((rows, half), f32)
            for c0 in range(0, chans, group):
                lhs = jnp.concatenate(
                    [sig_v[r, :, (c0 + c) * patch : (c0 + c + 1) * patch] for c in range(group)],
                    axis=0,
                )
                ys = jnp.dot(lhs, w, preferred_element_type=f32)
                for c in range(group):
                    y = ys[c * rows : (c + 1) * rows] + embed[c0 + c : c0 + c + 1, cs]
                    t = jnp.tanh(y * (GELU_A + GELU_B * (y * y)))
                    total = total + (y + y * t)
            total = total * (0.5 / CH)
            part[r, :, cs] = total
            send_p[r, :, cs] = total.astype(bf16)
            return carry

        lax.fori_loop(0, 2, col_step, 0)

        @pl.when(r == 0)
        def _():
            pl.semaphore_wait(barrier, n)

        part_copy(r).start()

    def norm_step(r):
        part_copy(r).wait_recv()
        pooled = part[r] + recv_p[r].astype(f32)
        part[r] = pooled
        center = pooled - jnp.mean(pooled, axis=-1, keepdims=True)
        spread = jnp.mean(center * center, axis=-1, keepdims=True)
        normed[r] = (center * lax.rsqrt(spread + 1e-05) * gain[...]).astype(bf16)

    lane_block = lax.broadcasted_iota(jnp.int32, (256, 256), 0) // HD
    sub_block = lax.broadcasted_iota(jnp.int32, (256, 256), 1) // HD
    means = jnp.where(lane_block == sub_block, 1.0 / HD, 0.0).astype(bf16)

    def unit(x):
        outs = []
        for b in range(share // 256):
            y = x[:, b * 256 : (b + 1) * 256]
            ms = jnp.dot((y * y).astype(bf16), means, preferred_element_type=f32)
            outs.append((y * lax.rsqrt(ms + 1e-06)).astype(bf16))
        return jnp.concatenate(outs, axis=1)

    def project(p):
        lo, hi = PIECES[p]
        b, rs = span(p)
        if p == 0:
            loads[1].wait()
        x = normed[lo:hi].reshape((hi - lo) * rows, width)
        for i in range(3):
            y = jnp.dot(x, qkv_v[i], preferred_element_type=f32)
            y = unit(y) if i < 2 else y.astype(bf16)
            for g in range(n):
                send_z[b, g, i, rs] = y[:, g * pair : (g + 1) * pair]
        for dest in others:
            z_send(p, dest).start()
        recv_z[b, :, me, rs] = send_z[b, me, :, rs]

    def front(t, carry):
        @pl.when(t < GRAIN)
        def _():
            patch_step(t)

        @pl.when(t >= DELAY)
        def _():
            norm_step(t - DELAY)

        for p in range(len(PIECES)):
            @pl.when(t - DELAY == PIECES[p][1] - 1)
            def _(p=p):
                project(p)

        return carry

    lax.fori_loop(0, GRAIN + DELAY, front, 0)

    count = n * size
    valid_len = lengths[0]
    low = lax.broadcasted_iota(jnp.int32, (count, pair), 1) < HD
    local = lax.broadcasted_iota(jnp.int32, (count, pair), 0)
    place = (local // size) * tok + local % size

    def arrive(b):
        for p in range(len(PIECES)):
            if PIECES[p][0] // per_block == b:
                for src in others:
                    z_recv(p, src).wait_recv()
        q = recv_z[b, 0].reshape(count, pair)
        v = recv_z[b, 2].reshape(count, pair)
        ok = jnp.where(place + b * size < valid_len, 1.0, 0.0)
        v = v.astype(f32) * ok
        zero = jnp.zeros_like(q)
        qz[0, b] = jnp.where(low, q, zero)
        qz[1, b] = jnp.where(low, zero, q)
        rhs[0, b] = jnp.where(low, v, ok).astype(bf16)
        rhs[1, b] = jnp.where(low, ok, v).astype(bf16)

    scales = [temp[2 * me + h] * (HD**-0.5 * LOG2E) for h in range(2)]

    def attend(i, k0, k1, first):
        keys = recv_z[k0:k1, 1].reshape((k1 - k0) * count, pair)
        for h in range(2):
            s = lax.dot_general(
                qz[h, i], keys, (((1,), (1,)), ((), ())), preferred_element_type=f32
            )
            e = jnp.exp2(s * scales[h]).astype(bf16)
            o = jnp.dot(
                e, rhs[h, k0:k1].reshape((k1 - k0) * count, pair), preferred_element_type=f32
            )
            if first:
                acc[h, i] = o
            else:
                acc[h, i] += o

    def finish(i):
        a0, a1 = acc[0, i], acc[1, i]
        num = jnp.where(low, a0, a1)
        den = pltpu.roll(jnp.where(low, a1, a0), HD, 1)
        den = jnp.where(place + i * size < valid_len, den, 1.0)
        send_a[i] = (num / den).astype(bf16).reshape(n, size, pair)
        for dest in others:
            a_send(i, dest).start()
        recv_a[i, me] = send_a[i, me]

    for b in range(blocks):
        arrive(b)
        for i in range(b):
            attend(i, b, b + 1, False)
            if b == blocks - 1:
                finish(i)
        attend(b, 0, b + 1, True)
    finish(blocks - 1)

    loads[2].wait()
    theirs = pl.ds(pl.multiple_of(other * share, share), share)
    mine = pl.ds(pl.multiple_of(col * share, share), share)
    for i in range(blocks):
        for src in others:
            a_recv(i, src).wait_recv()
        a = jnp.concatenate([recv_a[i, g] for g in range(n)], axis=1)
        send_b[i] = jnp.dot(a, ow_v[:, theirs], preferred_element_type=f32).astype(bf16)
        b_copy(i).start()
        own = jnp.dot(a, ow_v[:, mine], preferred_element_type=f32)
        pooled = part[i * per_block : (i + 1) * per_block, :, mine].reshape(size, share)
        own_v[i] = own + pooled
    for i in range(blocks):
        b_copy(i).wait_recv()
        pos = me * tok + i * size + lax.broadcasted_iota(jnp.int32, (size, share), 0)
        total = own_v[i] + recv_b[i].astype(f32)
        out[0, i * size : (i + 1) * size, :] = jnp.where(pos < valid_len, total, 0.0).astype(bf16)

    for r in range(GRAIN):
        part_copy(r).wait_send()
    for dest in others:
        for p in range(len(PIECES)):
            z_send(p, dest).wait_send()
        for i in range(blocks):
            a_send(i, dest).wait_send()
    for i in range(blocks):
        b_copy(i).wait_send()


def split_body(n, lengths, head_temp, signal, patch_weight, chan_embed, gain, qkv_weight, out_weight):
    _, tok, samples = signal.shape
    rows = tok // GRAIN
    patch, width = patch_weight.shape
    share = qkv_weight.shape[2]
    blocks = 4
    size = tok // blocks
    pair = 2 * HD
    f32, bf16 = jnp.float32, jnp.bfloat16
    vmem = pl.BlockSpec(memory_space=pltpu.VMEM)
    smem = pl.BlockSpec(memory_space=pltpu.SMEM)
    anyw = pl.BlockSpec(memory_space=pl.ANY)
    dma = pltpu.SemaphoreType.DMA
    return pl.pallas_call(
        functools.partial(split_kernel, n),
        out_shape=jax.ShapeDtypeStruct((1, tok, share), bf16),
        in_specs=[smem, smem, anyw, anyw, vmem, vmem, anyw, anyw],
        out_specs=vmem,
        scratch_shapes=[
            pltpu.VMEM((GRAIN, rows, samples), bf16),
            pltpu.VMEM((patch, width), bf16),
            pltpu.VMEM(qkv_weight.shape, bf16),
            pltpu.VMEM(out_weight.shape, bf16),
            pltpu.VMEM((GRAIN, rows, width), f32),
            pltpu.VMEM((GRAIN, rows, width), bf16),
            pltpu.VMEM((GRAIN, rows, width), bf16),
            pltpu.VMEM((GRAIN, rows, width), bf16),
            pltpu.VMEM((blocks, n, 3, size, pair), bf16),
            pltpu.VMEM((blocks, 3, n, size, pair), bf16),
            pltpu.VMEM((2, blocks, n * size, pair), bf16),
            pltpu.VMEM((2, blocks, n * size, pair), bf16),
            pltpu.VMEM((2, blocks, n * size, pair), f32),
            pltpu.VMEM((blocks, n, size, pair), bf16),
            pltpu.VMEM((blocks, n, size, pair), bf16),
            pltpu.VMEM((blocks, size, share), f32),
            pltpu.VMEM((blocks, size, share), bf16),
            pltpu.VMEM((blocks, size, share), bf16),
            dma((3,)),
            dma((GRAIN,)),
            dma((GRAIN,)),
            dma((GRAIN,)),
            dma((len(PIECES), n)),
            dma((len(PIECES), n)),
            dma((blocks, n)),
            dma((blocks, n)),
            dma((blocks,)),
            dma((blocks,)),
        ],
        compiler_params=pltpu.CompilerParams(
            collective_id=1, has_side_effects=True, vmem_limit_bytes=56 * 1024 * 1024
        ),
    )(lengths, head_temp, signal, patch_weight, chan_embed, gain, qkv_weight, out_weight)


def body(n, signal, lengths, patch_weight, chan_embed, ln_gain, qkv_weight, head_temp, out_weight):
    _, tok, samples = signal.shape
    rows = tok // CHUNKS
    patch, width = patch_weight.shape
    share = qkv_weight.shape[2]
    heads = head_temp.shape[0]
    full = WINDOW // tok
    reach = min(full, n - 1)
    slots = 2 * reach + 1
    f32, bf16 = jnp.float32, jnp.bfloat16
    vmem = pl.BlockSpec(memory_space=pltpu.VMEM)
    smem = pl.BlockSpec(memory_space=pltpu.SMEM)
    anyw = pl.BlockSpec(memory_space=pl.ANY)
    dma = pltpu.SemaphoreType.DMA
    if n > 1 and n * tok <= WINDOW + 1 and heads == 2 * n and tok % 256 == 0:
        return split_body(
            n, lengths, head_temp, signal, patch_weight, chan_embed, ln_gain.reshape(1, width),
            qkv_weight, out_weight,
        )
    return pl.pallas_call(
        functools.partial(kernel, n, reach, n - 1 >= full),
        out_shape=jax.ShapeDtypeStruct((1, tok, share), bf16),
        in_specs=[smem, smem, anyw, anyw, vmem, vmem, anyw, anyw],
        out_specs=vmem,
        scratch_shapes=[
            pltpu.VMEM((LOADS, tok // LOADS, samples), bf16),
            pltpu.VMEM((patch, width), bf16),
            pltpu.VMEM(qkv_weight.shape, bf16),
            pltpu.VMEM(out_weight.shape, bf16),
            pltpu.VMEM((CHUNKS, rows, width), f32),
            pltpu.VMEM((CHUNKS, rows, width), bf16),
            pltpu.VMEM((CHUNKS, rows, width), bf16),
            pltpu.VMEM((slots, CHUNKS, rows, width), bf16),
            pltpu.VMEM((heads, tok, 2 * HD), bf16),
            pltpu.VMEM((heads, tok, 2 * HD), f32),
            pltpu.VMEM((tok, share), bf16),
            pltpu.VMEM((2, tok // 2, share), bf16),
            pltpu.VMEM((2, tok // 2, share), bf16),
            dma((3,)),
            dma((LOADS,)),
            dma((CHUNKS,)),
            dma((CHUNKS,)),
            dma((slots, ITEMS)),
            dma((slots, ITEMS)),
            dma((slots, SPLIT)),
            dma((slots, SPLIT)),
            dma((2,)),
            dma((2,)),
        ],
        compiler_params=pltpu.CompilerParams(
            collective_id=0, has_side_effects=True, vmem_limit_bytes=56 * 1024 * 1024
        ),
    )(
        lengths, head_temp, signal, patch_weight, chan_embed, ln_gain.reshape(1, width),
        qkv_weight, out_weight,
    )


def solution(mesh):
    return jax.shard_map(
        functools.partial(body, mesh.shape["tm"]),
        mesh=mesh,
        in_specs=(
            P(("groups", "night"), "tm", "chan"),
            P(("groups", "night")),
            P(),
            P("chan", None),
            P(),
            P(None, None, "chan"),
            P("chan"),
            P("chan", None),
        ),
        out_specs=P(("groups", "night"), "tm", "chan"),
        check_vma=False,
    )
```

```python
import functools
import math

import jax
import jax.numpy as jnp
from jax import lax
from jax.experimental import pallas as pl
from jax.experimental.pallas import tpu as pltpu
from jax.sharding import PartitionSpec as P

CH = 32
HD = 64
WINDOW = 1024
LOADS = 4
CHUNKS = 8
SPLIT = 3
ITEMS = CHUNKS - SPLIT
LAG = 2
MESH = pl.DeviceIdType.MESH
GELU_A = math.sqrt(2.0 / math.pi)
GELU_B = GELU_A * 0.044715
LOG2E = math.log2(math.e)


def kernel(
    n, reach, far,
    lengths, temp, signal, patch_w, embed, gain, qkv_w, out_w,
    out,
    sig_v, pw_v, qkv_v, ow_v, part, send_p, recv_p, win, qz, acc, att, send_b, recv_b,
    load_sem, sig_sem, ps_sem, pr_sem, zs_sem, zr_sem, xs_sem, xr_sem, bs_sem, br_sem,
):
    me = lax.axis_index("tm")
    col = lax.axis_index("chan")
    other = 1 - col
    load_rows = sig_v.shape[1]
    tok = load_rows * LOADS
    rows = tok // CHUNKS
    per_load = CHUNKS // LOADS
    width = pw_v.shape[1]
    share = qkv_v.shape[2]
    heads = share // HD
    pairs = heads // 2
    patch = pw_v.shape[0]
    chans = embed.shape[0]
    f32, bf16 = jnp.float32, jnp.bfloat16

    def sig_copy(r):
        return pltpu.make_async_copy(
            signal.at[0, pl.ds(r * load_rows, load_rows), :], sig_v.at[r], sig_sem.at[r]
        )

    loads = [
        pltpu.make_async_copy(patch_w, pw_v, load_sem.at[0]),
        pltpu.make_async_copy(qkv_w, qkv_v, load_sem.at[1]),
        pltpu.make_async_copy(out_w, ow_v, load_sem.at[2]),
    ]
    barrier = pltpu.get_barrier_semaphore()
    pl.semaphore_signal(barrier, inc=1, device_id={"chan": other}, device_id_type=MESH)

    @pl.when(me > 0)
    def _():
        pl.semaphore_signal(barrier, inc=1, device_id={"tm": me - 1}, device_id_type=MESH)

    @pl.when(me < n - 1)
    def _():
        pl.semaphore_signal(barrier, inc=1, device_id={"tm": me + 1}, device_id_type=MESH)

    loads[0].start()
    for r in range(LOADS):
        sig_copy(r).start()
    loads[1].start()
    loads[2].start()

    def part_copy(r):
        return pltpu.make_async_remote_copy(
            src_ref=send_p.at[r], dst_ref=recv_p.at[r], send_sem=ps_sem.at[r],
            recv_sem=pr_sem.at[r], device_id={"chan": other}, device_id_type=MESH,
        )

    def slot_of(side, d):
        return 2 * (d - 1) + side + 1

    def source(side, d):
        return me - d if side == 0 else me + d

    def held(side, d):
        s = source(side, d)
        return (s >= 0) & (s < n)

    def sends(side, d):
        nxt = me + 1 if side == 0 else me - 1
        return held(side, d - 1) & (nxt >= 0) & (nxt < n)

    def row_of(j):
        return jnp.where(j < SPLIT, 2 * j + col, j + SPLIT)

    def z_copy(side, d, j):
        src = jnp.where(d == 1, 0, slot_of(side, d - 1))
        dst = slot_of(side, d)
        nxt = me + 1 if side == 0 else me - 1
        r = row_of(j)
        return pltpu.make_async_remote_copy(
            src_ref=win.at[src, r], dst_ref=win.at[dst, r], send_sem=zs_sem.at[dst, j],
            recv_sem=zr_sem.at[dst, j], device_id={"tm": nxt}, device_id_type=MESH,
        )

    def x_copy(slot, r, j):
        return pltpu.make_async_remote_copy(
            src_ref=win.at[slot, r], dst_ref=win.at[slot, r], send_sem=xs_sem.at[slot, j],
            recv_sem=xr_sem.at[slot, j], device_id={"chan": other}, device_id_type=MESH,
        )

    loads[0].wait()

    def patch_step(r):
        sig_copy(r).wait()
        half = width // 2

        def col_step(b, carry):
            cs = pl.ds(pl.multiple_of(b * half, half), half)
            w = pw_v[:, cs]
            total = jnp.zeros((load_rows, half), f32)
            for c0 in range(0, chans, 4):
                lhs = jnp.concatenate(
                    [sig_v[r, :, (c0 + c) * patch : (c0 + c + 1) * patch] for c in range(4)], axis=0
                )
                y4 = jnp.dot(lhs, w, preferred_element_type=f32)
                for c in range(4):
                    y = y4[c * load_rows : (c + 1) * load_rows] + embed[c0 + c : c0 + c + 1, cs]
                    t = jnp.tanh(y * (GELU_A + GELU_B * (y * y)))
                    total = total + (y + y * t)
            total = total * (0.5 / CH)
            for i in range(per_load):
                piece = total[i * rows : (i + 1) * rows]
                part[r * per_load + i, :, cs] = piece
                send_p[r * per_load + i, :, cs] = piece.astype(bf16)
            return carry

        lax.fori_loop(0, 2, col_step, 0)

        @pl.when(r == 0)
        def _():
            peers = 1 + jnp.where(me > 0, 1, 0) + jnp.where(me < n - 1, 1, 0)
            pl.semaphore_wait(barrier, peers)

        for i in range(per_load):
            part_copy(r * per_load + i).start()

    def norm_step(r):
        part_copy(r).wait_recv()
        pooled = part[r] + recv_p[r].astype(f32)
        part[r] = pooled
        center = pooled - jnp.mean(pooled, axis=-1, keepdims=True)
        spread = jnp.mean(center * center, axis=-1, keepdims=True)
        win[0, r] = (center * lax.rsqrt(spread + 1e-05) * gain[...]).astype(bf16)

        relay_out(r, 1)

    def handled(r):
        return (r >= 2 * SPLIT) | (lax.rem(r, 2) == col)

    def item_of(r):
        return jnp.where(r < 2 * SPLIT, r // 2, r - SPLIT)

    def relay_out(r, d):
        for side in range(2):
            @pl.when(handled(r) & sends(side, d))
            def _(side=side):
                z_copy(side, d, item_of(r)).start()

    def load_loop(r, carry):
        patch_step(r)
        return carry

    lax.fori_loop(0, LOADS, load_loop, 0)

    lane_block = lax.broadcasted_iota(jnp.int32, (256, 256), 0) // HD
    sub_block = lax.broadcasted_iota(jnp.int32, (256, 256), 1) // HD
    means = jnp.where(lane_block == sub_block, 1.0 / HD, 0.0).astype(bf16)
    low = lax.broadcasted_iota(jnp.int32, (tok, 2 * HD), 1) < HD

    def unit(x):
        outs = []
        for b in range(share // 256):
            y = x[:, b * 256 : (b + 1) * 256]
            ms = jnp.dot((y * y).astype(bf16), means, preferred_element_type=f32)
            outs.append((y * lax.rsqrt(ms + 1e-06)).astype(bf16))
        return jnp.concatenate(outs, axis=1)

    def project_queries():
        loads[1].wait()
        q = unit(jnp.dot(win[0].reshape(tok, width), qkv_v[0], preferred_element_type=f32))
        for p in range(pairs):
            qp = q[:, p * 2 * HD : (p + 1) * 2 * HD]
            zero = jnp.zeros_like(qp)
            qz[2 * p] = jnp.where(low, qp, zero)
            qz[2 * p + 1] = jnp.where(low, zero, qp)

    acc[...] = jnp.zeros_like(acc)
    valid_len = lengths[0]

    def attend(slot, src):
        x = win[slot].reshape(tok, width)
        k = unit(jnp.dot(x, qkv_v[1], preferred_element_type=f32))
        v = jnp.dot(x, qkv_v[2], preferred_element_type=f32)
        key_pos = src * tok + lax.broadcasted_iota(jnp.int32, (tok, 2 * HD), 0)
        ok = jnp.where(key_pos < valid_len, 1.0, 0.0)
        for p in range(pairs):
            kp = k[:, p * 2 * HD : (p + 1) * 2 * HD]
            vp = v[:, p * 2 * HD : (p + 1) * 2 * HD] * ok
            for h in range(2):
                rhs = jnp.where(low, vp, ok) if h == 0 else jnp.where(low, ok, vp)
                s = lax.dot_general(
                    qz[2 * p + h], kp, (((1,), (1,)), ((), ())), preferred_element_type=f32
                )
                e = jnp.exp2(s * (temp[2 * p + h] * (HD**-0.5 * LOG2E)))
                if far:
                    gap = (me - src) * tok + (
                        lax.broadcasted_iota(jnp.int32, (tok, tok), 0)
                        - lax.broadcasted_iota(jnp.int32, (tok, tok), 1)
                    )
                    e = jnp.where(jnp.abs(gap) <= WINDOW, e, 0.0)
                acc[2 * p + h] += jnp.dot(
                    e.astype(bf16), rhs.astype(bf16), preferred_element_type=f32
                )

    def relay(d, r):
        for side in range(2):
            @pl.when(handled(r) & held(side, d))
            def _(side=side):
                z_copy(side, d, item_of(r)).wait_recv()
                if d < reach:
                    @pl.when(sends(side, d + 1))
                    def _():
                        z_copy(side, d + 1, item_of(r)).start()

                @pl.when(r < 2 * SPLIT)
                def _():
                    x_copy(slot_of(side, d), r, item_of(r)).start()

    def attend_at(dist):
        def slot_step(i, c):
            src = jnp.where(i == 0, me - dist, me + dist)
            slot = jnp.where(dist == 0, 0, 2 * (dist - 1) + i + 1)

            @pl.when((src >= 0) & (src < n) & ((dist > 0) | (i == 0)))
            def _():
                @pl.when(dist > 0)
                def _():
                    for j in range(SPLIT):
                        x_copy(slot, 2 * j + other, j).wait_recv()

                attend(slot, src)

            return c

        lax.fori_loop(0, 2, slot_step, 0)

    def event(t, carry):
        @pl.when(t < CHUNKS)
        def _():
            norm_step(t)

        for d in range(1, reach + 1):
            r = t - LAG * d

            @pl.when((r >= 0) & (r < CHUNKS))
            def _(d=d, r=r):
                relay(d, r)

        late = t - CHUNKS + 1

        @pl.when((late >= 0) & (lax.rem(late, LAG) == 0))
        def _():
            @pl.when(late == 0)
            def _():
                project_queries()

            attend_at(late // LAG)

        return carry

    lax.fori_loop(0, CHUNKS + LAG * reach, event, 0)

    query_pos = me * tok + lax.broadcasted_iota(jnp.int32, (tok, 2 * HD), 0)
    live = query_pos < valid_len
    for p in range(pairs):
        a0, a1 = acc[2 * p], acc[2 * p + 1]
        num = jnp.where(low, a0, a1)
        den = pltpu.roll(jnp.where(low, a1, a0), HD, 1)
        den = jnp.where(live, den, 1.0)
        att[:, p * 2 * HD : (p + 1) * 2 * HD] = (num / den).astype(bf16)

    loads[2].wait()
    theirs = pl.ds(pl.multiple_of(other * share, share), share)
    mine = pl.ds(pl.multiple_of(col * share, share), share)

    def branch_copy(b):
        return pltpu.make_async_remote_copy(
            src_ref=send_b.at[b], dst_ref=recv_b.at[b], send_sem=bs_sem.at[b],
            recv_sem=br_sem.at[b], device_id={"chan": other}, device_id_type=MESH,
        )

    for b in range(2):
        a = att[b * (tok // 2) : (b + 1) * (tok // 2), :]
        send_b[b] = jnp.dot(a, ow_v[:, theirs], preferred_element_type=f32).astype(bf16)
        branch_copy(b).start()
    own = jnp.dot(att[...], ow_v[:, mine], preferred_element_type=f32)
    own = own + part[:, :, mine].reshape(tok, share)
    for b in range(2):
        rs = slice(b * (tok // 2), (b + 1) * (tok // 2))
        branch_copy(b).wait_recv()
        pos = me * tok + b * (tok // 2) + lax.broadcasted_iota(jnp.int32, (tok // 2, share), 0)
        total = own[rs] + recv_b[b].astype(f32)
        out[0, rs, :] = jnp.where(pos < valid_len, total, 0.0).astype(bf16)

    for r in range(CHUNKS):
        part_copy(r).wait_send()
    for b in range(2):
        branch_copy(b).wait_send()

    def drain(d, carry):
        for side in range(2):
            @pl.when(sends(side, d))
            def _(side=side):
                for j in range(ITEMS):
                    z_copy(side, d, j).wait_send()

            @pl.when(held(side, d))
            def _(side=side):
                for j in range(SPLIT):
                    x_copy(slot_of(side, d), 2 * j + col, j).wait_send()

        return carry

    lax.fori_loop(1, reach + 1, drain, 0)


GRAIN = 8
PIECES = ((0, 1), (1, 2), (2, 4), (4, 6), (6, 8))
DELAY = 3
AHEAD = 3


def split_kernel(
    n,
    lengths, temp, signal, patch_w, embed_w, gain_w, qkv_w, out_w,
    out,
    sig_v, pw_v, embed, gain, qkv_v, ow_v, part, send_p, recv_p, normed, send_z, recv_z, qz, rhs, acc,
    send_a, recv_a, own_v, send_b, recv_b,
    load_sem, sig_sem, ps_sem, pr_sem, zs_sem, zr_sem, as_sem, ar_sem, bs_sem, br_sem,
):
    me = lax.axis_index("tm")
    col = lax.axis_index("chan")
    other = 1 - col
    rows = sig_v.shape[1]
    tok = rows * GRAIN
    width = pw_v.shape[1]
    share = qkv_v.shape[2]
    patch = pw_v.shape[0]
    chans = embed.shape[0]
    blocks = recv_z.shape[0]
    size = tok // blocks
    per_block = GRAIN // blocks
    pair = 2 * HD
    f32, bf16 = jnp.float32, jnp.bfloat16

    def sig_copy(r):
        return pltpu.make_async_copy(
            signal.at[0, pl.ds(r * rows, rows), :], sig_v.at[r], sig_sem.at[r]
        )

    loads = [
        pltpu.make_async_copy(patch_w, pw_v, load_sem.at[0]),
        pltpu.make_async_copy(out_w, ow_v, load_sem.at[1]),
        pltpu.make_async_copy(embed_w, embed, load_sem.at[2]),
        pltpu.make_async_copy(gain_w, gain, load_sem.at[3]),
    ]

    def qkv_load(i):
        return pltpu.make_async_copy(qkv_w.at[i], qkv_v.at[i], load_sem.at[4 + i])

    barrier = pltpu.get_barrier_semaphore()
    pl.semaphore_signal(barrier, inc=1, device_id={"chan": other}, device_id_type=MESH)
    for k in range(1, n):
        pl.semaphore_signal(
            barrier, inc=1, device_id={"tm": lax.rem(me + k, n)}, device_id_type=MESH
        )
    loads[0].start()
    sig_copy(0).start()
    loads[2].start()
    loads[3].start()
    for r in range(1, AHEAD):
        sig_copy(r).start()

    def part_copy(r):
        return pltpu.make_async_remote_copy(
            src_ref=send_p.at[r], dst_ref=recv_p.at[r], send_sem=ps_sem.at[r],
            recv_sem=pr_sem.at[r], device_id={"chan": other}, device_id_type=MESH,
        )

    def span(p):
        b, g = PIECES[p][0] // per_block, PIECES[p][0] % per_block
        return b, pl.ds(g * rows, (PIECES[p][1] - PIECES[p][0]) * rows)

    def z_send(p, dest):
        b, rs = span(p)
        return pltpu.make_async_remote_copy(
            src_ref=send_z.at[b, dest, :, rs], dst_ref=recv_z.at[b, :, me, rs],
            send_sem=zs_sem.at[p, dest], recv_sem=zr_sem.at[p, me],
            device_id={"tm": dest}, device_id_type=MESH,
        )

    def z_recv(p, src):
        b, rs = span(p)
        return pltpu.make_async_remote_copy(
            src_ref=send_z.at[b, src, :, rs], dst_ref=recv_z.at[b, :, src, rs],
            send_sem=zs_sem.at[p, src], recv_sem=zr_sem.at[p, src],
            device_id={"tm": src}, device_id_type=MESH,
        )

    def a_send(i, dest):
        return pltpu.make_async_remote_copy(
            src_ref=send_a.at[i, dest], dst_ref=recv_a.at[i, me], send_sem=as_sem.at[i, dest],
            recv_sem=ar_sem.at[i, me], device_id={"tm": dest}, device_id_type=MESH,
        )

    def a_recv(i, src):
        return pltpu.make_async_remote_copy(
            src_ref=send_a.at[i, src], dst_ref=recv_a.at[i, src], send_sem=as_sem.at[i, src],
            recv_sem=ar_sem.at[i, src], device_id={"tm": src}, device_id_type=MESH,
        )

    def b_copy(i):
        return pltpu.make_async_remote_copy(
            src_ref=send_b.at[i], dst_ref=recv_b.at[i], send_sem=bs_sem.at[i],
            recv_sem=br_sem.at[i], device_id={"chan": other}, device_id_type=MESH,
        )

    others = [lax.rem(me + k, n) for k in range(1, n)]
    loads[0].wait()
    loads[2].wait()
    loads[3].wait()
    group = 256 // rows

    def patch_step(r):
        sig_copy(r).wait()

        @pl.when(r + AHEAD < GRAIN)
        def _():
            sig_copy(r + AHEAD).start()

        for i in range(3):
            @pl.when(r == i)
            def _(i=i):
                qkv_load(i).start()

        @pl.when(r == 3)
        def _():
            loads[1].start()

        half = width // 2
        for b in range(2):
            cs = slice(b * half, (b + 1) * half)
            w = pw_v[:, cs]
            total = jnp.zeros((rows, half), f32)
            for c0 in range(0, chans, group):
                lhs = jnp.concatenate(
                    [sig_v[r, :, (c0 + c) * patch : (c0 + c + 1) * patch] for c in range(group)],
                    axis=0,
                )
                ys = jnp.dot(lhs, w, preferred_element_type=f32)
                for c in range(group):
                    y = ys[c * rows : (c + 1) * rows] + embed[c0 + c : c0 + c + 1, cs]
                    t = jnp.tanh(y * (GELU_A + GELU_B * (y * y)))
                    total = total + (y + y * t)
            total = total * (0.5 / CH)
            part[r, :, cs] = total
            send_p[r, :, cs] = total.astype(bf16)

        @pl.when(r == 0)
        def _():
            pl.semaphore_wait(barrier, n)

        part_copy(r).start()

    def norm_step(r):
        part_copy(r).wait_recv()
        pooled = part[r] + recv_p[r].astype(f32)
        part[r] = pooled
        center = pooled - jnp.mean(pooled, axis=-1, keepdims=True)
        spread = jnp.mean(center * center, axis=-1, keepdims=True)
        normed[r] = (center * lax.rsqrt(spread + 1e-05) * gain[...]).astype(bf16)

    lane_block = lax.broadcasted_iota(jnp.int32, (256, 256), 0) // HD
    sub_block = lax.broadcasted_iota(jnp.int32, (256, 256), 1) // HD
    means = jnp.where(lane_block == sub_block, 1.0 / HD, 0.0).astype(bf16)

    def unit(x):
        outs = []
        for b in range(share // 256):
            y = x[:, b * 256 : (b + 1) * 256]
            ms = jnp.dot((y * y).astype(bf16), means, preferred_element_type=f32)
            outs.append((y * lax.rsqrt(ms + 1e-06)).astype(bf16))
        return jnp.concatenate(outs, axis=1)

    def project(p):
        lo, hi = PIECES[p]
        b, rs = span(p)
        x = normed[lo:hi].reshape((hi - lo) * rows, width)
        for i in range(3):
            if p == 0:
                qkv_load(i).wait()
            y = jnp.dot(x, qkv_v[i], preferred_element_type=f32)
            y = unit(y) if i < 2 else y.astype(bf16)
            for g in range(n):
                send_z[b, g, i, rs] = y[:, g * pair : (g + 1) * pair]
        for dest in others:
            z_send(p, dest).start()
        recv_z[b, :, me, rs] = send_z[b, me, :, rs]

    def front(t, carry):
        @pl.when(t < GRAIN)
        def _():
            patch_step(t)

        @pl.when(t >= DELAY)
        def _():
            norm_step(t - DELAY)

        for p in range(len(PIECES)):
            @pl.when(t - DELAY == PIECES[p][1] - 1)
            def _(p=p):
                project(p)

        return carry

    lax.fori_loop(0, GRAIN + DELAY, front, 0)

    count = n * size
    valid_len = lengths[0]
    low = lax.broadcasted_iota(jnp.int32, (count, pair), 1) < HD
    local = lax.broadcasted_iota(jnp.int32, (count, pair), 0)
    place = (local // size) * tok + local % size

    def arrive(b):
        for p in range(len(PIECES)):
            if PIECES[p][0] // per_block == b:
                for src in others:
                    z_recv(p, src).wait_recv()
        q = recv_z[b, 0].reshape(count, pair)
        v = recv_z[b, 2].reshape(count, pair)
        ok = jnp.where(place + b * size < valid_len, 1.0, 0.0)
        v = v.astype(f32) * ok
        zero = jnp.zeros_like(q)
        qz[0, b] = jnp.where(low, q, zero)
        qz[1, b] = jnp.where(low, zero, q)
        rhs[0, b] = jnp.where(low, v, ok).astype(bf16)
        rhs[1, b] = jnp.where(low, ok, v).astype(bf16)

    scales = [temp[2 * me + h] * (HD**-0.5 * LOG2E) for h in range(2)]

    def attend(i, k0, k1, first):
        keys = recv_z[k0:k1, 1].reshape((k1 - k0) * count, pair)
        for h in range(2):
            s = lax.dot_general(
                qz[h, i], keys, (((1,), (1,)), ((), ())), preferred_element_type=f32
            )
            e = jnp.exp2(s * scales[h]).astype(bf16)
            o = jnp.dot(
                e, rhs[h, k0:k1].reshape((k1 - k0) * count, pair), preferred_element_type=f32
            )
            if first:
                acc[h, i] = o
            else:
                acc[h, i] += o

    def finish(i):
        a0, a1 = acc[0, i], acc[1, i]
        num = jnp.where(low, a0, a1)
        den = pltpu.roll(jnp.where(low, a1, a0), HD, 1)
        den = jnp.where(place + i * size < valid_len, den, 1.0)
        send_a[i] = (num / den).astype(bf16).reshape(n, size, pair)
        for dest in others:
            a_send(i, dest).start()
        recv_a[i, me] = send_a[i, me]

    for b in range(blocks):
        arrive(b)
        for i in range(b):
            attend(i, b, b + 1, False)
            if b == blocks - 1:
                finish(i)
        attend(b, 0, b + 1, True)
    finish(blocks - 1)

    loads[1].wait()
    theirs = pl.ds(pl.multiple_of(other * share, share), share)
    mine = pl.ds(pl.multiple_of(col * share, share), share)
    for i in range(blocks):
        for src in others:
            a_recv(i, src).wait_recv()
        a = jnp.concatenate([recv_a[i, g] for g in range(n)], axis=1)
        send_b[i] = jnp.dot(a, ow_v[:, theirs], preferred_element_type=f32).astype(bf16)
        b_copy(i).start()
        own = jnp.dot(a, ow_v[:, mine], preferred_element_type=f32)
        pooled = part[i * per_block : (i + 1) * per_block, :, mine].reshape(size, share)
        own_v[i] = own + pooled
    for i in range(blocks):
        b_copy(i).wait_recv()
        pos = me * tok + i * size + lax.broadcasted_iota(jnp.int32, (size, share), 0)
        total = own_v[i] + recv_b[i].astype(f32)
        out[0, i * size : (i + 1) * size, :] = jnp.where(pos < valid_len, total, 0.0).astype(bf16)

    for r in range(GRAIN):
        part_copy(r).wait_send()
    for dest in others:
        for p in range(len(PIECES)):
            z_send(p, dest).wait_send()
        for i in range(blocks):
            a_send(i, dest).wait_send()
    for i in range(blocks):
        b_copy(i).wait_send()


def split_body(n, lengths, head_temp, signal, patch_weight, chan_embed, gain, qkv_weight, out_weight):
    _, tok, samples = signal.shape
    rows = tok // GRAIN
    patch, width = patch_weight.shape
    share = qkv_weight.shape[2]
    blocks = 4
    size = tok // blocks
    pair = 2 * HD
    f32, bf16 = jnp.float32, jnp.bfloat16
    vmem = pl.BlockSpec(memory_space=pltpu.VMEM)
    smem = pl.BlockSpec(memory_space=pltpu.SMEM)
    anyw = pl.BlockSpec(memory_space=pl.ANY)
    dma = pltpu.SemaphoreType.DMA
    return pl.pallas_call(
        functools.partial(split_kernel, n),
        out_shape=jax.ShapeDtypeStruct((1, tok, share), bf16),
        in_specs=[smem, smem, anyw, anyw, anyw, anyw, anyw, anyw],
        out_specs=vmem,
        scratch_shapes=[
            pltpu.VMEM((GRAIN, rows, samples), bf16),
            pltpu.VMEM((patch, width), bf16),
            pltpu.VMEM(chan_embed.shape, f32),
            pltpu.VMEM((1, width), f32),
            pltpu.VMEM(qkv_weight.shape, bf16),
            pltpu.VMEM(out_weight.shape, bf16),
            pltpu.VMEM((GRAIN, rows, width), f32),
            pltpu.VMEM((GRAIN, rows, width), bf16),
            pltpu.VMEM((GRAIN, rows, width), bf16),
            pltpu.VMEM((GRAIN, rows, width), bf16),
            pltpu.VMEM((blocks, n, 3, size, pair), bf16),
            pltpu.VMEM((blocks, 3, n, size, pair), bf16),
            pltpu.VMEM((2, blocks, n * size, pair), bf16),
            pltpu.VMEM((2, blocks, n * size, pair), bf16),
            pltpu.VMEM((2, blocks, n * size, pair), f32),
            pltpu.VMEM((blocks, n, size, pair), bf16),
            pltpu.VMEM((blocks, n, size, pair), bf16),
            pltpu.VMEM((blocks, size, share), f32),
            pltpu.VMEM((blocks, size, share), bf16),
            pltpu.VMEM((blocks, size, share), bf16),
            dma((7,)),
            dma((GRAIN,)),
            dma((GRAIN,)),
            dma((GRAIN,)),
            dma((len(PIECES), n)),
            dma((len(PIECES), n)),
            dma((blocks, n)),
            dma((blocks, n)),
            dma((blocks,)),
            dma((blocks,)),
        ],
        compiler_params=pltpu.CompilerParams(
            collective_id=1, has_side_effects=True, vmem_limit_bytes=56 * 1024 * 1024
        ),
    )(lengths, head_temp, signal, patch_weight, chan_embed, gain, qkv_weight, out_weight)


def body(n, signal, lengths, patch_weight, chan_embed, ln_gain, qkv_weight, head_temp, out_weight):
    _, tok, samples = signal.shape
    rows = tok // CHUNKS
    patch, width = patch_weight.shape
    share = qkv_weight.shape[2]
    heads = head_temp.shape[0]
    full = WINDOW // tok
    reach = min(full, n - 1)
    slots = 2 * reach + 1
    f32, bf16 = jnp.float32, jnp.bfloat16
    vmem = pl.BlockSpec(memory_space=pltpu.VMEM)
    smem = pl.BlockSpec(memory_space=pltpu.SMEM)
    anyw = pl.BlockSpec(memory_space=pl.ANY)
    dma = pltpu.SemaphoreType.DMA
    if n > 1 and n * tok <= WINDOW + 1 and heads == 2 * n and tok % 256 == 0:
        return split_body(
            n, lengths, head_temp, signal, patch_weight, chan_embed, ln_gain.reshape(1, width),
            qkv_weight, out_weight,
        )
    return pl.pallas_call(
        functools.partial(kernel, n, reach, n - 1 >= full),
        out_shape=jax.ShapeDtypeStruct((1, tok, share), bf16),
        in_specs=[smem, smem, anyw, anyw, vmem, vmem, anyw, anyw],
        out_specs=vmem,
        scratch_shapes=[
            pltpu.VMEM((LOADS, tok // LOADS, samples), bf16),
            pltpu.VMEM((patch, width), bf16),
            pltpu.VMEM(qkv_weight.shape, bf16),
            pltpu.VMEM(out_weight.shape, bf16),
            pltpu.VMEM((CHUNKS, rows, width), f32),
            pltpu.VMEM((CHUNKS, rows, width), bf16),
            pltpu.VMEM((CHUNKS, rows, width), bf16),
            pltpu.VMEM((slots, CHUNKS, rows, width), bf16),
            pltpu.VMEM((heads, tok, 2 * HD), bf16),
            pltpu.VMEM((heads, tok, 2 * HD), f32),
            pltpu.VMEM((tok, share), bf16),
            pltpu.VMEM((2, tok // 2, share), bf16),
            pltpu.VMEM((2, tok // 2, share), bf16),
            dma((3,)),
            dma((LOADS,)),
            dma((CHUNKS,)),
            dma((CHUNKS,)),
            dma((slots, ITEMS)),
            dma((slots, ITEMS)),
            dma((slots, SPLIT)),
            dma((slots, SPLIT)),
            dma((2,)),
            dma((2,)),
        ],
        compiler_params=pltpu.CompilerParams(
            collective_id=0, has_side_effects=True, vmem_limit_bytes=56 * 1024 * 1024
        ),
    )(
        lengths, head_temp, signal, patch_weight, chan_embed, ln_gain.reshape(1, width),
        qkv_weight, out_weight,
    )


def solution(mesh):
    return jax.shard_map(
        functools.partial(body, mesh.shape["tm"]),
        mesh=mesh,
        in_specs=(
            P(("groups", "night"), "tm", "chan"),
            P(("groups", "night")),
            P(),
            P("chan", None),
            P(),
            P(None, None, "chan"),
            P("chan"),
            P("chan", None),
        ),
        out_specs=P(("groups", "night"), "tm", "chan"),
        check_vma=False,
    )
```
